32 devices in a mesh: cond: 4 (over z), ty: 2 (over y), tx: 4 (over x, core).
Axes of the slice: x: 2, y: 2, z: 4, core: 2. Of those that a mesh axis runs over, the one named last changes fastest.
Arguments:
- mask_logits: float32 [1024, 2048], P('ty', 'tx'), may hold values from -8 to 8
- target_layout: int32 [1024, 2048], P('ty', 'tx'), may hold values 0 or 1
- density_weights: int32 [1024, 2048], P('ty', 'tx'), may hold values from 0 to 3, as said below
- socs_kernels: float32 [4, 12, 2, 24, 24], P('cond'), may hold values from -3 to 3
Outputs:
- logits_new: float32 [1024, 2048], P('ty', 'tx')
- mask_next: bfloat16 [1024, 2048], P('ty', 'tx')
The draws below stay inside these ranges and needn't reach their ends.
Inputs may be any that keep to these rules, and one draw needn't show every extreme that they name: `density_weights`: weights are constant zero over exactly a quarter, rounded down, of the 512 x 512 tiles; elsewhere each pixel's weight is drawn afresh.
All inputs are finite; a program needn't handle non-finite values. No bound on the sum of `target_layout` on one device may be relied on, other than what follows from the above.
Results may differ from the reference program's by a relative error of at most 0.001.
Values sent between devices are 32-bit elements; how exact they have to be, the bound alone decides.
A program may use at most 64 MiB of HBM per device.

```python
import math
import jax
import jax.numpy as jnp
from jax import lax

TILE = 512
MARGIN = 128
BAND = 24
KERN = 12
COND = 4
ROWS = 1024
COLS = 2048
N_TY = 2
N_TX = 4


def draw_density_weights(key, part):
    key_rank, key_level = jax.random.split(jax.random.fold_in(key, 11))
    tiles_down = ROWS // TILE
    tiles_across = COLS // TILE
    tile_count = tiles_down * tiles_across
    ranking = jax.random.permutation(key_rank, tile_count)
    active = (ranking >= tile_count // 4).astype(jnp.int32).reshape(tiles_down, 1, tiles_across, 1)
    levels = jax.random.randint(key_level, (tiles_down, TILE, tiles_across, TILE), 0, 4, dtype=jnp.int32)
    return (levels * active).reshape(ROWS, COLS)


def set_ends(drawn, own_key, smallest, largest):
    dims = drawn.shape
    place = [jax.random.randint(jax.random.fold_in(own_key, axis), (), 0, dims[axis]) for axis in range(len(dims))]
    drawn = drawn.at[tuple(place)].set(smallest)
    longest = dims.index(max(dims))
    place[longest] = (place[longest] + 1) % dims[longest]
    return drawn.at[tuple(place)].set(largest)


def shard_levels(rng, extent, cuts, least, high):
    gain = 1.0
    for dim, blocks in cuts:
        steps = jax.random.uniform(jax.random.fold_in(jax.random.fold_in(rng, 6), dim), (blocks,), jnp.float32, least / len(cuts), high / len(cuts))
        gain = gain * jnp.repeat(jnp.exp(steps), extent[dim] // blocks).reshape((-1,) + (1,) * (len(extent) - 1 - dim))
    return gain


def noise(stream_key, shape, scale, most, cuts=(), kind=jnp.bfloat16):
    entries = jax.random.normal(stream_key, shape, jnp.float32) * scale
    if len(cuts) > 0:
        entries = shard_levels(stream_key, shape, cuts, -0.22, 0.18) * entries
    return jnp.clip(entries, min=-most, max=most).astype(kind)


def setup_inputs(seed: int = 0) -> dict:
    seeds = jax.random.split(jax.random.key(seed), 5)
    mask_logits = noise(seeds[0], (ROWS, COLS), 1.5, 8.0, ((0, 2), (1, 4)), jnp.float32)
    target_layout = set_ends((jax.random.randint(seeds[1], (ROWS, COLS), 0, 5) < 2).astype(jnp.int32), jax.random.fold_in(seeds[1], 1), 0, 1)
    density_weights = draw_density_weights(jax.random.fold_in(seeds[4], 71), 0)
    socs_kernels = noise(seeds[3], (COND, KERN, 2, BAND, BAND), ((2 * KERN) ** -0.5), 3.0, ((0, 4),), jnp.float32)
    return dict(mask_logits=mask_logits, target_layout=target_layout, density_weights=density_weights, socs_kernels=socs_kernels)


STEEPNESS = 6.0
THRESHOLD = 0.25
STEP_SIZE = 4.0

def matmul_hi(first, second):
    return jnp.dot(first, second, precision=lax.Precision.HIGHEST, preferred_element_type=jnp.float32)

def band_tables(count_rows, offset, length, band_size):
    positions = jnp.arange(count_rows, dtype=jnp.int32) + offset
    frequency = jnp.arange(band_size, dtype=jnp.int32) - band_size // 2
    turn_count = jnp.mod(positions[:, None] * frequency[None, :], length).astype(jnp.float32)
    angles = turn_count * (2.0 * math.pi / length)
    return (jnp.cos(angles), jnp.sin(angles))

def tile_loss(window, layout, weight_vals, kernels_here):
    length = window.shape[0]
    win_cos, win_sin = band_tables(length, 0, length, BAND)
    tile_cos, tile_sin = band_tables(TILE, MARGIN, length, BAND)
    normalizer = 1.0 / (length * length)
    cos_rows = matmul_hi(win_cos.T, window)
    sin_rows = matmul_hi(win_sin.T, window)
    spec_re = (matmul_hi(cos_rows, win_cos) - matmul_hi(sin_rows, win_sin)) * normalizer
    spec_im = -(matmul_hi(cos_rows, win_sin) + matmul_hi(sin_rows, win_cos)) * normalizer
    intensity = jnp.zeros((TILE, TILE), jnp.float32)
    for kernel_index in range(KERN):
        kern_re = kernels_here[kernel_index, 0]
        kern_im = kernels_here[kernel_index, 1]
        amp_re = kern_re * spec_re - kern_im * spec_im
        amp_im = kern_re * spec_im + kern_im * spec_re
        half_re = matmul_hi(amp_re, tile_cos.T) - matmul_hi(amp_im, tile_sin.T)
        half_im = matmul_hi(amp_re, tile_sin.T) + matmul_hi(amp_im, tile_cos.T)
        field_re = matmul_hi(tile_cos, half_re) - matmul_hi(tile_sin, half_im)
        field_im = matmul_hi(tile_cos, half_im) + matmul_hi(tile_sin, half_re)
        intensity = intensity + field_re * field_re + field_im * field_im
    resist = jax.nn.sigmoid(STEEPNESS * (intensity - THRESHOLD))
    return jnp.sum(weight_vals * (resist - layout) ** 2)

def reference(mask_logits, target_layout, density_weights, socs_kernels):
    mask_now = 0.5 * (1.0 + jnp.tanh(mask_logits))
    padded = jnp.pad(mask_now, MARGIN)
    length = TILE + 2 * MARGIN
    tile_count = N_TY * N_TX

    def visit_tile(accumulated, tile_index):
        row_start = tile_index // N_TX * TILE
        col_start = tile_index % N_TX * TILE
        window = lax.dynamic_slice(padded, (row_start, col_start), (length, length))
        layout = lax.dynamic_slice(target_layout, (row_start, col_start), (TILE, TILE)).astype(jnp.float32)
        weight_vals = lax.dynamic_slice(density_weights, (row_start, col_start), (TILE, TILE)).astype(jnp.float32)
        window_grad = jnp.zeros((length, length), jnp.float32)
        for condition in range(COND):
            window_grad = window_grad + jax.grad(tile_loss)(window, layout, weight_vals, socs_kernels[condition])
        previous = lax.dynamic_slice(accumulated, (row_start, col_start), (length, length))
        return (lax.dynamic_update_slice(accumulated, previous + window_grad, (row_start, col_start)), None)
    accumulated, _ = lax.scan(visit_tile, jnp.zeros_like(padded), jnp.arange(tile_count, dtype=jnp.int32))
    mask_grad = accumulated[MARGIN:MARGIN + ROWS, MARGIN:MARGIN + COLS]
    logits_new = mask_logits - STEP_SIZE * mask_grad * (2.0 * mask_now * (1.0 - mask_now))
    mask_next = (0.5 * (1.0 + jnp.tanh(logits_new))).astype(jnp.bfloat16)
    return (logits_new, mask_next)
```

```python
import functools
import math

import jax
import jax.numpy as jnp
import numpy as np
from jax import lax
from jax.experimental import pallas as pl
from jax.experimental.pallas import tpu as pltpu
from jax.sharding import PartitionSpec as P

MARGIN = 128
BAND = 24
STEEPNESS = 6.0
THRESHOLD = 0.25
STEP_SIZE = 4.0
LANES = 128
MESH = pl.DeviceIdType.MESH
OFFSETS = [(dr, dc) for dr in (-1, 0, 1) for dc in (-1, 0, 1)]
BF = jnp.bfloat16
F32 = jnp.float32


def waves(positions, frequency, period):
    turns = np.mod(np.outer(positions, frequency), period).astype(np.float64)
    return np.cos(turns * (2 * math.pi / period)), np.sin(turns * (2 * math.pi / period))


def halves(table):
    table = np.asarray(table, np.float32)
    high = table.astype(BF)
    return high, (table - high.astype(np.float32)).astype(BF)


def place(rows, cols, *pieces):
    out = np.zeros((rows, cols))
    for top, left, piece in pieces:
        out[top : top + piece.shape[0], left : left + piece.shape[1]] = piece
    return out


def make_tables(tile, margin, band):
    length = tile + 2 * margin
    norm = 1.0 / (length * length)
    freq = np.arange(band) - band // 2
    grid = -(-(2 * band - 1) // 16) * 16
    shifted = []
    for step in (-1, 0, 1):
        spots = np.arange(tile) + margin - step * tile
        inside = ((spots >= 0) & (spots < length))[:, None]
        cos, sin = waves(spots, freq, length)
        shifted.append((cos * inside, sin * inside))
    col_cos = np.concatenate([c for c, _ in shifted], 1)
    col_sin = np.concatenate([s for _, s in shifted], 1)
    fwd_cols = place(tile, 2 * LANES, (0, 0, col_cos), (0, LANES, col_sin))
    fwd_rows = norm * np.concatenate(
        [np.block([[c.T, -s.T], [-s.T, -c.T]]) for c, s in shifted], 0
    )
    ec, es = waves(np.arange(grid), freq, grid)
    right_re = place(LANES, 2 * LANES, (0, 0, ec.T), (0, LANES, es.T))
    right_im = place(LANES, 2 * LANES, (0, 0, -es.T), (0, LANES, ec.T))
    left = np.block([[ec, -es], [es, ec]])
    right_back = place(
        2 * LANES, 2 * LANES,
        (0, 0, ec), (0, LANES, -es), (LANES, 0, es), (LANES, LANES, ec),
    )
    orders = np.arange(1, band)
    turn = (np.arange(tile) + margin)[:, None] / length - np.arange(grid)[None, :] / grid
    interp = (1 + 2 * np.cos(2 * math.pi * turn[:, :, None] * orders).sum(-1)) / grid
    ih, il = halves(interp)
    lh, ll = halves(left)
    th, tl = halves(left.T)
    ih128 = place(tile, LANES, (0, 0, ih.astype(np.float64)))
    il128 = place(tile, LANES, (0, 0, il.astype(np.float64)))
    back_rows = np.concatenate([np.concatenate([c, -s], 1) for c, s in shifted], 1)
    bh, bl = halves(back_rows)
    back_cols = place(LANES, 2 * tile, (0, 0, col_cos.T), (0, tile, col_sin.T))
    front = dict(
        fch=halves(fwd_cols)[0], fcl=halves(fwd_cols)[1],
        frh=halves(fwd_rows)[0], frl=halves(fwd_rows)[1],
        rrh=halves(right_re)[0], rrl=halves(right_re)[1],
        rih=halves(right_im)[0], ril=halves(right_im)[1],
        left=np.concatenate([lh, lh, ll], 1),
        wth=ih128.T.astype(BF), wtl=il128.T.astype(BF),
        wcat=np.concatenate([ih, ih, il], 1),
        wn=np.concatenate([ih128, il128], 1).astype(BF),
        lt=np.concatenate([th, th, tl], 1),
        rbh=halves(right_back)[0], rbl=halves(right_back)[1],
    )
    back = dict(
        bch=halves(back_cols)[0], bcl=halves(back_cols)[1],
        brow=np.concatenate([bh, bh, bl], 1),
    )
    return front, back, grid


def split(x):
    high = x.astype(BF)
    return high, (x - high.astype(F32)).astype(BF)


def mm(a, b):
    return jnp.dot(a, b, preferred_element_type=F32)


def mm3(ah, al, bh, bl):
    return mm(ah, bh) + mm(ah, bl) + mm(al, bh)


def front_kernel(names, grid, n_k, *refs):
    n_tab = len(names)
    logits_hbm, target_hbm, weight_hbm, kern_hbm = refs[:4]
    tab_hbm = dict(zip(names, refs[4 : 4 + n_tab]))
    out_ref = refs[4 + n_tab]
    rest = refs[5 + n_tab :]
    logits, target, weight, kern = rest[:4]
    tab = dict(zip(names, rest[4 : 4 + n_tab]))
    (kpad, send1, recv1, zs_own, recv_c, zs_sum, recv2,
     load_sem, s1, r1, sc, rc, s2, r2) = rest[4 + n_tab :]

    tile = logits.shape[0]
    band = kern.shape[-1]
    both = 2 * band
    length = tile + 2 * MARGIN
    norm = 1.0 / (length * length)
    n_ty, n_tx, n_c = lax.axis_size("ty"), lax.axis_size("tx"), lax.axis_size("cond")
    ty, tx, me = lax.axis_index("ty"), lax.axis_index("tx"), lax.axis_index("cond")

    loads = {}
    order = ["logits", "fch", "fcl", "frh", "frl", "kern"]
    order += [n for n in names if n not in order] + ["target", "weight"]
    src = dict(tab_hbm, logits=logits_hbm, target=target_hbm, weight=weight_hbm, kern=kern_hbm)
    dst = dict(tab, logits=logits, target=target, weight=weight, kern=kern)
    for i, name in enumerate(order):
        loads[name] = pltpu.make_async_copy(src[name], dst[name], load_sem.at[i])
        loads[name].start()

    def exists(dr, dc):
        row, col = ty + dr, tx + dc
        return (row >= 0) & (row < n_ty) & (col >= 0) & (col < n_tx)

    around = [(i, o) for i, o in enumerate(OFFSETS) if o != (0, 0)]
    barrier = pltpu.get_barrier_semaphore()
    for _, (dr, dc) in around:
        @pl.when(exists(dr, dc))
        def _():
            pl.semaphore_signal(
                barrier, inc=1, device_id={"ty": ty + dr, "tx": tx + dc}, device_id_type=MESH
            )
    for j in range(1, n_c):
        pl.semaphore_signal(
            barrier, inc=1, device_id={"cond": lax.rem(me + j, n_c)}, device_id_type=MESH
        )
    for i, (dr, dc) in around:
        @pl.when(jnp.logical_not(exists(-dr, -dc)))
        def _():
            recv1[i] = jnp.zeros(recv1.shape[1:], F32)
            recv2[i] = jnp.zeros(recv2.shape[1:], F32)
    kpad[...] = jnp.zeros(kpad.shape, F32)

    loads["logits"].wait()
    loads["fch"].wait()
    loads["fcl"].wait()
    mask = 0.5 * (1.0 + jnp.tanh(logits[...]))
    mh, ml = split(mask)
    fch = tab["fch"][...]
    proj = mm(mh, fch) + mm(ml, fch) + mm(mh, tab["fcl"][...])
    ph, pw = split(jnp.concatenate([proj[:, :LANES], proj[:, LANES:]], 0))
    loads["frh"].wait()
    loads["frl"].wait()
    share = mm3(tab["frh"][...], tab["frl"][...], ph, pw)
    for i, (dr, dc) in enumerate(OFFSETS):
        rows = share[(dr + 1) * both : (dr + 2) * both]
        send1[i] = rows if dc == -1 else pltpu.roll(rows, LANES - (dc + 1) * band, 1)

    peers = n_c - 1
    for _, (dr, dc) in around:
        peers = peers + exists(dr, dc).astype(jnp.int32)
    pl.semaphore_wait(barrier, peers)

    def to_neighbour(source, dest, ss, rs, i, dr, dc):
        return pltpu.make_async_remote_copy(
            src_ref=source, dst_ref=dest.at[i], send_sem=ss.at[i], recv_sem=rs.at[i],
            device_id={"ty": ty + dr, "tx": tx + dc}, device_id_type=MESH,
        )

    for i, (dr, dc) in around:
        @pl.when(exists(dr, dc))
        def _():
            to_neighbour(send1.at[i], recv1, s1, r1, i, dr, dc).start()
    loads["kern"].wait()
    kpad[:, :, :, :band] = kern[0]
    for name in order:
        if name not in ("logits", "fch", "fcl", "frh", "frl", "kern"):
            loads[name].wait()
    spec = send1[4]
    for i, (dr, dc) in around:
        @pl.when(exists(-dr, -dc))
        def _():
            to_neighbour(send1.at[i], recv1, s1, r1, i, dr, dc).wait_recv()
    for i, _ in around:
        spec = spec + recv1[i]

    sr, si = spec[:band], spec[band:]
    kr, ki = kpad[:, 0], kpad[:, 1]
    ar = (kr * sr - ki * si).reshape(n_k * band, LANES)
    ai = (kr * si + ki * sr).reshape(n_k * band, LANES)
    arh, arl = split(ar)
    aih, ail = split(ai)
    half = mm3(arh, arl, tab["rrh"][...], tab["rrl"][...]) + mm3(
        aih, ail, tab["rih"][...], tab["ril"][...]
    )
    stacked = jnp.concatenate(
        [
            jnp.concatenate(
                [
                    half[k * band : (k + 1) * band, :LANES],
                    half[k * band : (k + 1) * band, LANES:],
                ],
                0,
            )
            for k in range(n_k)
        ],
        1,
    )
    hh, hl = split(stacked)
    field = mm(tab["left"][...], jnp.concatenate([hh, hl, hh], 0))
    squares = field * field
    coarse = jnp.zeros((grid, LANES), F32)
    for k in range(n_k):
        cut = squares[:, k * LANES : (k + 1) * LANES]
        coarse = coarse + cut[:grid] + cut[grid:]
    ch, cl = split(coarse)
    uh, ul = split(mm3(ch, cl, tab["wth"][...], tab["wtl"][...]))
    ustack = jnp.concatenate([uh, ul, uh], 0)

    wn = tab["wn"][...]
    chunk = min(tile, 128)
    col_parts = []
    for row in range(0, tile, chunk):
        intensity = mm(tab["wcat"][row : row + chunk], ustack)
        th = jnp.tanh((0.5 * STEEPNESS) * (intensity - THRESHOLD))
        resist = 0.5 + 0.5 * th
        layout = target[row : row + chunk].astype(F32)
        vals = weight[row : row + chunk].astype(F32)
        gain = (STEEPNESS * 2.0) * vals * (resist - layout) * resist * (1.0 - resist)
        gh, gl = split(gain)
        wide = mm(gh, wn)
        col_parts.append(wide[:, :LANES] + wide[:, LANES:] + mm(gl, wn[:, :LANES]))
    yh, yl = split(jnp.concatenate(col_parts, 0))
    gcoarse = 2.0 * mm3(tab["wth"][:grid], tab["wtl"][:grid], yh, yl)

    gpair = jnp.concatenate([gcoarse, gcoarse], 0)
    slope = jnp.concatenate(
        [gpair * field[:, k * LANES : (k + 1) * LANES] for k in range(n_k)], 1
    )
    dh, dl = split(slope)
    u = mm(tab["lt"][...], jnp.concatenate([dh, dl, dh], 0))
    uu = jnp.concatenate(
        [
            jnp.concatenate(
                [
                    u[:band, k * LANES : (k + 1) * LANES],
                    u[band:, k * LANES : (k + 1) * LANES],
                ],
                1,
            )
            for k in range(n_k)
        ],
        0,
    )
    vh, vl = split(uu)
    za = mm3(vh, vl, tab["rbh"][...], tab["rbl"][...])
    za_re = za[:, :LANES].reshape(n_k, band, LANES)
    za_im = za[:, LANES:].reshape(n_k, band, LANES)
    zs_own[:band] = norm * jnp.sum(kr * za_re + ki * za_im, axis=0)
    zs_own[band:] = norm * jnp.sum(kr * za_im - ki * za_re, axis=0)

    over = []
    for j in range(1, n_c):
        copy = pltpu.make_async_remote_copy(
            src_ref=zs_own, dst_ref=recv_c.at[j], send_sem=sc.at[j], recv_sem=rc.at[j],
            device_id={"cond": lax.rem(me + j, n_c)}, device_id_type=MESH,
        )
        copy.start()
        over.append(copy)
    total = zs_own[...]
    for j, copy in enumerate(over):
        copy.wait_recv()
        total = total + recv_c[j + 1]
    zs_sum[...] = total
    for i, (dr, dc) in around:
        @pl.when(exists(dr, dc))
        def _():
            to_neighbour(zs_sum, recv2, s2, r2, i, dr, dc).start()
    recv2[4] = total
    for i, (dr, dc) in around:
        @pl.when(exists(-dr, -dc))
        def _():
            to_neighbour(zs_sum, recv2, s2, r2, i, dr, dc).wait_recv()
    for er in (-1, 0, 1):
        acc = jnp.zeros((both, LANES), F32)
        for ec in (-1, 0, 1):
            block = recv2[OFFSETS.index((-er, -ec))]
            acc = acc + (block if ec == -1 else pltpu.roll(block, (ec + 1) * band, 1))
        out_ref[(er + 1) * both : (er + 2) * both] = acc

    for i, (dr, dc) in around:
        @pl.when(exists(dr, dc))
        def _():
            to_neighbour(send1.at[i], recv1, s1, r1, i, dr, dc).wait_send()
            to_neighbour(zs_sum, recv2, s2, r2, i, dr, dc).wait_send()
    for copy in over:
        copy.wait_send()


def back_kernel(band, z_ref, bch, bcl, brow, logits, new_ref, next_ref, stack):
    tile = logits.shape[1]
    both = 2 * band

    @pl.when(pl.program_id(0) == 0)
    def _():
        zh, zl = split(z_ref[...])
        wide = mm3(zh, zl, bch[...], bcl[...])
        rows = []
        for a in range(3):
            re = wide[a * both : a * both + band]
            im = wide[a * both + band : (a + 1) * both]
            rows += [re[:, :tile] - im[:, tile:], re[:, tile:] + im[:, :tile]]
        vh, vl = split(jnp.concatenate(rows, 0))
        n = 3 * both
        stack[:n] = vh
        stack[n : 2 * n] = vl
        stack[2 * n :] = vh

    grad = mm(brow[...], stack[...])
    x = logits[...]
    mask = 0.5 * (1.0 + jnp.tanh(x))
    new = x - STEP_SIZE * grad * (2.0 * mask * (1.0 - mask))
    new_ref[...] = new
    next_ref[...] = (0.5 * (1.0 + jnp.tanh(new))).astype(BF)


def per_device(mask_logits, target_layout, density_weights, socs_kernels):
    tile = mask_logits.shape[0]
    band = socs_kernels.shape[-1]
    n_k = socs_kernels.shape[1]
    n_c = lax.axis_size("cond")
    front, back, grid = make_tables(tile, MARGIN, band)
    names = list(front)
    both = 2 * band
    arrays = [mask_logits, target_layout, density_weights, socs_kernels]
    arrays += [jnp.asarray(front[n]) for n in names]
    dma = pltpu.SemaphoreType.DMA
    n_off = len(OFFSETS)
    zrow = pl.pallas_call(
        functools.partial(front_kernel, names, grid, n_k),
        out_shape=jax.ShapeDtypeStruct((3 * both, LANES), F32),
        in_specs=[pl.BlockSpec(memory_space=pl.ANY)] * len(arrays),
        out_specs=pl.BlockSpec(memory_space=pltpu.VMEM),
        scratch_shapes=[pltpu.VMEM(a.shape, a.dtype) for a in arrays]
        + [
            pltpu.VMEM((n_k, 2, band, LANES), F32),
            pltpu.VMEM((n_off, both, LANES), F32),
            pltpu.VMEM((n_off, both, LANES), F32),
            pltpu.VMEM((both, LANES), F32),
            pltpu.VMEM((n_c, both, LANES), F32),
            pltpu.VMEM((both, LANES), F32),
            pltpu.VMEM((n_off, both, LANES), F32),
            dma((len(arrays),)),
            dma((n_off,)),
            dma((n_off,)),
            dma((n_c,)),
            dma((n_c,)),
            dma((n_off,)),
            dma((n_off,)),
        ],
        compiler_params=pltpu.CompilerParams(
            collective_id=0, has_side_effects=True, vmem_limit_bytes=60 * 2**20
        ),
    )(*arrays)

    blocks = 4
    rows = tile // blocks
    whole = lambda shape: pl.BlockSpec(shape, lambda i: (0, 0))
    by_row = lambda width: pl.BlockSpec((rows, width), lambda i: (i, 0))
    return pl.pallas_call(
        functools.partial(back_kernel, band),
        grid=(blocks,),
        out_shape=(
            jax.ShapeDtypeStruct((tile, tile), F32),
            jax.ShapeDtypeStruct((tile, tile), BF),
        ),
        in_specs=[
            whole((3 * both, LANES)),
            whole(back["bch"].shape),
            whole(back["bcl"].shape),
            by_row(back["brow"].shape[1]),
            by_row(tile),
        ],
        out_specs=(by_row(tile), by_row(tile)),
        scratch_shapes=[pltpu.VMEM((9 * both, tile), BF)],
    )(zrow, jnp.asarray(back["bch"]), jnp.asarray(back["bcl"]), jnp.asarray(back["brow"]), mask_logits)


def solution(mesh):
    in_specs = (P("ty", "tx"), P("ty", "tx"), P("ty", "tx"), P("cond", None, None, None, None))
    out_specs = (P("ty", "tx"), P("ty", "tx"))
    return jax.shard_map(
        per_device, mesh=mesh, in_specs=in_specs, out_specs=out_specs, check_vma=False
    )
```

```python
import functools
import math

import jax
import jax.numpy as jnp
import numpy as np
from jax import lax
from jax.experimental import pallas as pl
from jax.experimental.pallas import tpu as pltpu
from jax.sharding import PartitionSpec as P

MARGIN = 128
BAND = 24
STEEPNESS = 6.0
THRESHOLD = 0.25
STEP_SIZE = 4.0
LANES = 128
MESH = pl.DeviceIdType.MESH
OFFSETS = [(dr, dc) for dr in (-1, 0, 1) for dc in (-1, 0, 1)]
BF = jnp.bfloat16
F32 = jnp.float32


def waves(positions, frequency, period):
    turns = np.mod(np.outer(positions, frequency), period).astype(np.float64)
    return np.cos(turns * (2 * math.pi / period)), np.sin(turns * (2 * math.pi / period))


def halves(table):
    table = np.asarray(table, np.float32)
    high = table.astype(BF)
    return high, (table - high.astype(np.float32)).astype(BF)


def place(rows, cols, *pieces):
    out = np.zeros((rows, cols))
    for top, left, piece in pieces:
        out[top : top + piece.shape[0], left : left + piece.shape[1]] = piece
    return out


def make_tables(tile, margin, band):
    length = tile + 2 * margin
    norm = 1.0 / (length * length)
    freq = np.arange(band) - band // 2
    grid = -(-(2 * band - 1) // 16) * 16
    shifted = []
    for step in (-1, 0, 1):
        spots = np.arange(tile) + margin - step * tile
        inside = ((spots >= 0) & (spots < length))[:, None]
        cos, sin = waves(spots, freq, length)
        shifted.append((cos * inside, sin * inside))
    col_cos = np.concatenate([c for c, _ in shifted], 1)
    col_sin = np.concatenate([s for _, s in shifted], 1)
    fwd_cols = place(tile, 2 * LANES, (0, 0, col_cos), (0, LANES, col_sin))
    fwd_rows = norm * np.concatenate(
        [np.block([[c.T, -s.T], [-s.T, -c.T]]) for c, s in shifted], 0
    )
    ec, es = waves(np.arange(grid), freq, grid)
    right_re = place(LANES, 2 * LANES, (0, 0, ec.T), (0, LANES, es.T))
    right_im = place(LANES, 2 * LANES, (0, 0, -es.T), (0, LANES, ec.T))
    left = np.block([[ec, -es], [es, ec]])
    right_back = place(
        2 * LANES, 2 * LANES,
        (0, 0, ec), (0, LANES, -es), (LANES, 0, es), (LANES, LANES, ec),
    )
    orders = np.arange(1, band)
    turn = (np.arange(tile) + margin)[:, None] / length - np.arange(grid)[None, :] / grid
    interp = (1 + 2 * np.cos(2 * math.pi * turn[:, :, None] * orders).sum(-1)) / grid
    ih, il = halves(interp)
    lh, ll = halves(left)
    th, tl = halves(left.T)
    ih128 = place(tile, LANES, (0, 0, ih.astype(np.float64)))
    il128 = place(tile, LANES, (0, 0, il.astype(np.float64)))
    back_rows = np.concatenate([np.concatenate([c, -s], 1) for c, s in shifted], 1)
    bh, bl = halves(back_rows)
    back_cols = place(LANES, 2 * tile, (0, 0, col_cos.T), (0, tile, col_sin.T))
    front = dict(
        fch=halves(fwd_cols)[0], fcl=halves(fwd_cols)[1],
        frh=halves(fwd_rows)[0], frl=halves(fwd_rows)[1],
        rrh=halves(right_re)[0], rrl=halves(right_re)[1],
        rih=halves(right_im)[0], ril=halves(right_im)[1],
        left=np.concatenate([lh, lh, ll], 1),
        wth=ih128.T.astype(BF), wtl=il128.T.astype(BF),
        wcat=np.concatenate([ih, ih, il], 1),
        wn=np.concatenate([ih128, il128], 1).astype(BF),
        lt=np.concatenate([th, th, tl], 1),
        rbh=halves(right_back)[0], rbl=halves(right_back)[1],
    )
    back = dict(
        bch=halves(back_cols)[0], bcl=halves(back_cols)[1],
        brow=np.concatenate([bh, bh, bl], 1),
    )
    return front, back, grid


def split(x):
    high = x.astype(BF)
    return high, (x - high.astype(F32)).astype(BF)


def mm(a, b):
    return jnp.dot(a, b, preferred_element_type=F32)


def mm3(ah, al, bh, bl):
    return mm(ah, bh) + mm(ah, bl) + mm(al, bh)


def roll(x, shift):
    shift = shift % LANES
    return x if shift == 0 else pltpu.roll(x, shift, 1)


def packing(band):
    groups = 2 * band // 8
    count = -(-groups * band // LANES)
    return count, -(-groups // count)


def by_slot(band, pieces):
    lane = lax.broadcasted_iota(jnp.int32, pieces[0].shape, 1)
    out = pieces[-1]
    for j in range(len(pieces) - 2, -1, -1):
        out = jnp.where(lane < (j + 1) * band, pieces[j], out)
    return out


def pack(rows, band, start):
    count, per = packing(band)
    groups = rows.shape[0] // 8
    packed = []
    for v in range(count):
        pieces = [
            roll(rows[8 * t : 8 * t + 8], (j - start) * band)
            for j, t in enumerate(range(v * per, min((v + 1) * per, groups)))
        ]
        packed.append(by_slot(band, pieces))
    return jnp.concatenate(packed, 0)


def unpack(blocks, band):
    _, per = packing(band)
    out = []
    for t in range(2 * band // 8):
        v, j = t // per, t % per
        out.append(by_slot(band, [roll(b[8 * v : 8 * v + 8], (i - j) * band) for i, b in enumerate(blocks)]))
    return jnp.concatenate(out, 0)


def front_kernel(names, grid, n_k, *refs):
    n_tab = len(names)
    logits_hbm, target_hbm, weight_hbm, kern_hbm = refs[:4]
    tab_hbm = dict(zip(names, refs[4 : 4 + n_tab]))
    late_hbm = refs[4 + n_tab : 7 + n_tab]
    out_ref, logits = refs[7 + n_tab : 9 + n_tab]
    late = refs[9 + n_tab : 12 + n_tab]
    rest = refs[12 + n_tab :]
    target, weight, kern = rest[:3]
    tab = dict(zip(names, rest[3 : 3 + n_tab]))
    (kpad, send1, recv1, zs_own, recv_c, zs_sum, recv2,
     load_sem, s1, r1, sc, rc, s2, r2) = rest[3 + n_tab :]

    tile = logits.shape[0]
    band = kern.shape[-1]
    both = 2 * band
    length = tile + 2 * MARGIN
    norm = 1.0 / (length * length)
    n_ty, n_tx, n_c = lax.axis_size("ty"), lax.axis_size("tx"), lax.axis_size("cond")
    ty, tx, me = lax.axis_index("ty"), lax.axis_index("tx"), lax.axis_index("cond")

    loads = {}
    order = ["logits", "fch", "fcl", "frh", "frl", "kern"]
    order += [n for n in names if n not in order] + ["target", "weight"]
    src = dict(tab_hbm, logits=logits_hbm, target=target_hbm, weight=weight_hbm, kern=kern_hbm)
    dst = dict(tab, logits=logits, target=target, weight=weight, kern=kern)
    for i, name in enumerate(order):
        loads[name] = pltpu.make_async_copy(src[name], dst[name], load_sem.at[i])
        loads[name].start()
    passed = [
        pltpu.make_async_copy(a, b, load_sem.at[len(order) + i])
        for i, (a, b) in enumerate(zip(late_hbm, late))
    ]
    for copy in passed:
        copy.start()

    def exists(dr, dc):
        row, col = ty + dr, tx + dc
        return (row >= 0) & (row < n_ty) & (col >= 0) & (col < n_tx)

    around = [(i, o) for i, o in enumerate(OFFSETS) if o != (0, 0)]
    barrier = pltpu.get_barrier_semaphore()
    for _, (dr, dc) in around:
        @pl.when(exists(dr, dc))
        def _():
            pl.semaphore_signal(
                barrier, inc=1, device_id={"ty": ty + dr, "tx": tx + dc}, device_id_type=MESH
            )
    for j in range(1, n_c):
        pl.semaphore_signal(
            barrier, inc=1, device_id={"cond": lax.rem(me + j, n_c)}, device_id_type=MESH
        )
    for i, (dr, dc) in around:
        @pl.when(jnp.logical_not(exists(-dr, -dc)))
        def _():
            recv1[i] = jnp.zeros(recv1.shape[1:], F32)
            recv2[i] = jnp.zeros(recv2.shape[1:], F32)
    kpad[...] = jnp.zeros(kpad.shape, F32)

    loads["logits"].wait()
    loads["fch"].wait()
    loads["fcl"].wait()
    mask = 0.5 * (1.0 + jnp.tanh(logits[...]))
    mh, ml = split(mask)
    fch = tab["fch"][...]
    proj = mm(mh, fch) + mm(ml, fch) + mm(mh, tab["fcl"][...])
    ph, pw = split(jnp.concatenate([proj[:, :LANES], proj[:, LANES:]], 0))
    loads["frh"].wait()
    loads["frl"].wait()
    share = mm3(tab["frh"][...], tab["frl"][...], ph, pw)
    for i, (dr, dc) in enumerate(OFFSETS):
        rows = share[(dr + 1) * both : (dr + 2) * both]
        send1[i] = pack(rows, band, dc + 1)

    peers = n_c - 1
    for _, (dr, dc) in around:
        peers = peers + exists(dr, dc).astype(jnp.int32)
    pl.semaphore_wait(barrier, peers)

    def to_neighbour(source, dest, ss, rs, i, dr, dc):
        return pltpu.make_async_remote_copy(
            src_ref=source, dst_ref=dest.at[i], send_sem=ss.at[i], recv_sem=rs.at[i],
            device_id={"ty": ty + dr, "tx": tx + dc}, device_id_type=MESH,
        )

    for i, (dr, dc) in around:
        @pl.when(exists(dr, dc))
        def _():
            to_neighbour(send1.at[i], recv1, s1, r1, i, dr, dc).start()
    loads["kern"].wait()
    kpad[:, :, :, :band] = kern[0]
    for name in order:
        if name not in ("logits", "fch", "fcl", "frh", "frl", "kern"):
            loads[name].wait()
    spec = send1[4]
    for i, (dr, dc) in around:
        @pl.when(exists(-dr, -dc))
        def _():
            to_neighbour(send1.at[i], recv1, s1, r1, i, dr, dc).wait_recv()
    for i, _ in around:
        spec = spec + recv1[i]

    spec = unpack([spec], band)
    sr, si = spec[:band], spec[band:]
    kr, ki = kpad[:, 0], kpad[:, 1]
    ar = (kr * sr - ki * si).reshape(n_k * band, LANES)
    ai = (kr * si + ki * sr).reshape(n_k * band, LANES)
    arh, arl = split(ar)
    aih, ail = split(ai)
    half = mm3(arh, arl, tab["rrh"][...], tab["rrl"][...]) + mm3(
        aih, ail, tab["rih"][...], tab["ril"][...]
    )
    stacked = jnp.concatenate(
        [
            jnp.concatenate(
                [
                    half[k * band : (k + 1) * band, :LANES],
                    half[k * band : (k + 1) * band, LANES:],
                ],
                0,
            )
            for k in range(n_k)
        ],
        1,
    )
    hh, hl = split(stacked)
    field = mm(tab["left"][...], jnp.concatenate([hh, hl, hh], 0))
    squares = field * field
    coarse = jnp.zeros((grid, LANES), F32)
    for k in range(n_k):
        cut = squares[:, k * LANES : (k + 1) * LANES]
        coarse = coarse + cut[:grid] + cut[grid:]
    ch, cl = split(coarse)
    uh, ul = split(mm3(ch, cl, tab["wth"][...], tab["wtl"][...]))
    ustack = jnp.concatenate([uh, ul, uh], 0)

    wn = tab["wn"][...]
    chunk = min(tile, 128)
    col_parts = []
    for row in range(0, tile, chunk):
        intensity = mm(tab["wcat"][row : row + chunk], ustack)
        th = jnp.tanh((0.5 * STEEPNESS) * (intensity - THRESHOLD))
        resist = 0.5 + 0.5 * th
        layout = target[row : row + chunk].astype(F32)
        vals = weight[row : row + chunk].astype(F32)
        gain = (STEEPNESS * 2.0) * vals * (resist - layout) * resist * (1.0 - resist)
        gh, gl = split(gain)
        wide = mm(gh, wn)
        col_parts.append(wide[:, :LANES] + wide[:, LANES:] + mm(gl, wn[:, :LANES]))
    yh, yl = split(jnp.concatenate(col_parts, 0))
    gcoarse = 2.0 * mm3(tab["wth"][:grid], tab["wtl"][:grid], yh, yl)

    gpair = jnp.concatenate([gcoarse, gcoarse], 0)
    slope = jnp.concatenate(
        [gpair * field[:, k * LANES : (k + 1) * LANES] for k in range(n_k)], 1
    )
    dh, dl = split(slope)
    u = mm(tab["lt"][...], jnp.concatenate([dh, dl, dh], 0))
    uu = jnp.concatenate(
        [
            jnp.concatenate(
                [
                    u[:band, k * LANES : (k + 1) * LANES],
                    u[band:, k * LANES : (k + 1) * LANES],
                ],
                1,
            )
            for k in range(n_k)
        ],
        0,
    )
    vh, vl = split(uu)
    za = mm3(vh, vl, tab["rbh"][...], tab["rbl"][...])
    za_re = za[:, :LANES].reshape(n_k, band, LANES)
    za_im = za[:, LANES:].reshape(n_k, band, LANES)
    zs_re = norm * jnp.sum(kr * za_re + ki * za_im, axis=0)
    zs_im = norm * jnp.sum(kr * za_im - ki * za_re, axis=0)
    zs_own[...] = pack(jnp.concatenate([zs_re, zs_im], 0), band, 0)

    over = []
    for j in range(1, n_c):
        copy = pltpu.make_async_remote_copy(
            src_ref=zs_own, dst_ref=recv_c.at[j], send_sem=sc.at[j], recv_sem=rc.at[j],
            device_id={"cond": lax.rem(me + j, n_c)}, device_id_type=MESH,
        )
        copy.start()
        over.append(copy)
    total = zs_own[...]
    for j, copy in enumerate(over):
        copy.wait_recv()
        total = total + recv_c[j + 1]
    zs_sum[...] = total
    for i, (dr, dc) in around:
        @pl.when(exists(dr, dc))
        def _():
            to_neighbour(zs_sum, recv2, s2, r2, i, dr, dc).start()
    recv2[4] = total
    for i, (dr, dc) in around:
        @pl.when(exists(-dr, -dc))
        def _():
            to_neighbour(zs_sum, recv2, s2, r2, i, dr, dc).wait_recv()
    for er in (-1, 0, 1):
        blocks = [recv2[OFFSETS.index((-er, -ec))] for ec in (-1, 0, 1)]
        out_ref[(er + 1) * both : (er + 2) * both] = unpack(blocks, band)

    for i, (dr, dc) in around:
        @pl.when(exists(dr, dc))
        def _():
            to_neighbour(send1.at[i], recv1, s1, r1, i, dr, dc).wait_send()
            to_neighbour(zs_sum, recv2, s2, r2, i, dr, dc).wait_send()
    for copy in over:
        copy.wait_send()
    for copy in passed:
        copy.wait()


def back_kernel(band, z_ref, logits, bch, bcl, brow, new_hbm, next_hbm, stack, new, nxt, sem):
    tile = logits.shape[1]
    both = 2 * band
    zh, zl = split(z_ref[...])
    wide = mm3(zh, zl, bch[...], bcl[...])
    rows = []
    for a in range(3):
        re = wide[a * both : a * both + band]
        im = wide[a * both + band : (a + 1) * both]
        rows += [re[:, :tile] - im[:, tile:], re[:, tile:] + im[:, :tile]]
    vh, vl = split(jnp.concatenate(rows, 0))
    n = 3 * both
    stack[:n] = vh
    stack[n : 2 * n] = vl
    stack[2 * n :] = vh

    chunk = min(tile, 128)
    copies = []
    for i in range(tile // chunk):
        part = slice(i * chunk, (i + 1) * chunk)
        grad = mm(brow[part], stack[...])
        x = logits[part]
        mask = 0.5 * (1.0 + jnp.tanh(x))
        value = x - STEP_SIZE * grad * (2.0 * mask * (1.0 - mask))
        new[part] = value
        nxt[part] = (0.5 * (1.0 + jnp.tanh(value))).astype(BF)
        for j, (buf, out) in enumerate(((new, new_hbm), (nxt, next_hbm))):
            copy = pltpu.make_async_copy(buf.at[part], out.at[part], sem.at[2 * i + j])
            copy.start()
            copies.append(copy)
    for copy in copies:
        copy.wait()


def per_device(mask_logits, target_layout, density_weights, socs_kernels):
    tile = mask_logits.shape[0]
    band = socs_kernels.shape[-1]
    n_k = socs_kernels.shape[1]
    n_c = lax.axis_size("cond")
    front, back, grid = make_tables(tile, MARGIN, band)
    names = list(front)
    both = 2 * band
    arrays = [mask_logits, target_layout, density_weights, socs_kernels]
    arrays += [jnp.asarray(front[n]) for n in names]
    late = [jnp.asarray(back[n]) for n in ("bch", "bcl", "brow")]
    in_vmem = pl.BlockSpec(memory_space=pltpu.VMEM)
    in_hbm = pl.BlockSpec(memory_space=pl.ANY)
    dma = pltpu.SemaphoreType.DMA
    n_off = len(OFFSETS)
    held = 8 * packing(band)[0]
    kept = pl.pallas_call(
        functools.partial(front_kernel, names, grid, n_k),
        out_shape=[pltpu.VMEM((3 * both, LANES), F32), pltpu.VMEM((tile, tile), F32)]
        + [pltpu.VMEM(a.shape, a.dtype) for a in late],
        in_specs=[in_hbm] * (len(arrays) + len(late)),
        out_specs=[in_vmem] * (2 + len(late)),
        scratch_shapes=[pltpu.VMEM(a.shape, a.dtype) for a in arrays[1:]]
        + [
            pltpu.VMEM((n_k, 2, band, LANES), F32),
            pltpu.VMEM((n_off, held, LANES), F32),
            pltpu.VMEM((n_off, held, LANES), F32),
            pltpu.VMEM((held, LANES), F32),
            pltpu.VMEM((n_c, held, LANES), F32),
            pltpu.VMEM((held, LANES), F32),
            pltpu.VMEM((n_off, held, LANES), F32),
            dma((len(arrays) + len(late),)),
            dma((n_off,)),
            dma((n_off,)),
            dma((n_c,)),
            dma((n_c,)),
            dma((n_off,)),
            dma((n_off,)),
        ],
        compiler_params=pltpu.CompilerParams(
            collective_id=0, has_side_effects=True, vmem_limit_bytes=56 * 2**20
        ),
    )(*arrays, *late)

    return pl.pallas_call(
        functools.partial(back_kernel, band),
        out_shape=(
            jax.ShapeDtypeStruct((tile, tile), F32),
            jax.ShapeDtypeStruct((tile, tile), BF),
        ),
        in_specs=[in_vmem] * 5,
        out_specs=(in_hbm, in_hbm),
        scratch_shapes=[
            pltpu.VMEM((9 * both, tile), BF),
            pltpu.VMEM((tile, tile), F32),
            pltpu.VMEM((tile, tile), BF),
            dma((2 * (tile // min(tile, 128)),)),
        ],
        compiler_params=pltpu.CompilerParams(vmem_limit_bytes=16 * 2**20),
    )(*kept)


def solution(mesh):
    in_specs = (P("ty", "tx"), P("ty", "tx"), P("ty", "tx"), P("cond", None, None, None, None))
    out_specs = (P("ty", "tx"), P("ty", "tx"))
    return jax.shard_map(
        per_device, mesh=mesh, in_specs=in_specs, out_specs=out_specs, check_vma=False
    )
```
